256 devices in a mesh: dp: 8 (over z), expert: 32 (over y, x, core).
Axes of the slice: x: 4, y: 4, z: 8, core: 2. Of those that a mesh axis runs over, the one named last changes fastest.
Arguments:
- tokens: bfloat16 [32768, 2048], P(('dp', 'expert')), may hold values from -6 to 6
- out_grad: bfloat16 [32768, 2048], P(('dp', 'expert')), may hold values from -6 to 6
- expert_ids: int32 [32768, 6], P(('dp', 'expert')), may hold values from 0 to 31, all different within a row; in each aligned block of 128 rows (0 to 127, 128 to 255, ...) at most 25 rows name the same one
- gate_weights: float32 [32768, 6], P(('dp', 'expert')), may hold values from 0.05 to 1
- trained: int32 [8], replicated, may hold values from 0 to 31, as said below
- w_in: bfloat16 [32, 2048, 1408], P('expert'), may hold values from -0.125 to 0.125
- w_down: bfloat16 [32, 704, 2048], P('expert'), may hold values from -0.21875 to 0.21875
- saved: bfloat16 [8, 32, 800, 1408], P('dp', 'expert'), may hold values from -6 to 6
Outputs:
- in_grad: bfloat16 [32768, 2048], P(('dp', 'expert'))
- weight_grad: bfloat16 [32, 2048, 2112], P('expert', 'dp')
The draws below stay inside these ranges and needn't reach their ends.
Inputs may be any that keep to these rules, and one draw needn't show every extreme that they name: `expert_ids`: among the 128 tokens of one device no expert is named more than 25 times, a bound that some block reaches; a token names 6 different experts. `trained`: 8 different expert ids; the ids 0 and 31 are always among them.
All inputs are finite; a program needn't handle non-finite values.
Results may differ from the reference program's by a relative error of at most 0.017.
Values may be sent and summed in bfloat16 or wider, within the bound.
A program may use at most 128 MiB of HBM per device.

```python
import math
import jax
import jax.numpy as jnp
import numpy as np
from jax import lax

D = 2048
FF = 704
TOP = 6
TOK_DEV = 128
EXPERTS = 32
CAP = 25
N_TRAIN = 8
TOKENS = 32768
N_DP = 8
N_EXPERT = 32
DEVICES = 256


def draw_trained(key, part):
    inner_key = jax.random.fold_in(key, 11)
    order_key = jax.random.fold_in(key, 23)
    middle = jax.random.permutation(inner_key, EXPERTS - 2)[:N_TRAIN - 2].astype(jnp.int32) + 1
    ends = jnp.array([0, EXPERTS - 1], dtype=jnp.int32)
    chosen = jnp.concatenate([ends, middle]).astype(jnp.int32)
    return jax.random.permutation(order_key, chosen).astype(jnp.int32)


def shard_levels(rng, shape, shards, least, high):
    factor_of, own = 1.0, jax.random.fold_in(rng, 6)
    for dim, parts in shards:
        steps = jnp.exp(jax.random.uniform(jax.random.fold_in(own, dim), (parts,), jnp.float32, least / len(shards), high / len(shards)))
        factor_of = factor_of * jnp.repeat(steps, shape[dim] // parts).reshape([-1 if axis == dim else 1 for axis in range(len(shape))])
    return factor_of


def deal_out(key, own, number, rows, amount, top, limit, lean):
    order = jax.random.permutation(key, amount)
    packed, common = portions_of(amount, rows * top, limit, lean, True), portions_of(amount, rows * top, limit, lean, False)
    places = jnp.arange(amount)

    def named(lengths, rotation):
        used = int((lengths > 0).sum())
        fixed = max(1, used // 4)
        moved = fixed + (places - fixed + rotation * (used - fixed)) % max(1, amount - fixed)
        return jnp.zeros((amount,), jnp.int32).at[order[jnp.where(places < fixed, places, moved)]].set(jnp.asarray(lengths, jnp.int32))

    lengths = jnp.where(number % 4 == 0, named(packed, number // 4), named(common, number - number // 4 - 1))
    mixed = jax.random.permutation(jax.random.fold_in(own, 3), amount)
    donor, sink = mixed[0:amount // 2 * 2:2], mixed[1:amount // 2 * 2:2]
    margin = jnp.minimum(lengths[donor] - 1, limit - lengths[sink]) // 2
    margin = jnp.where((donor == order[0]) | (sink == order[0]) | (lengths[sink] == 0), 0, jnp.maximum(margin, 0))
    moved = jax.random.randint(jax.random.fold_in(own, 4), (amount // 2,), 0, 1 << 20) % (margin + 1)
    lengths = lengths.at[donor].add(-moved).at[sink].add(moved)
    items = jnp.searchsorted(jnp.cumsum(lengths), jnp.arange(rows * top), side="right").astype(jnp.int32)
    listing = items.reshape(top, rows).T
    listing = listing[jax.random.permutation(jax.random.fold_in(own, 1), rows)]
    rotation = jax.random.randint(jax.random.fold_in(own, 2), (rows, 1), 0, top)
    return jnp.take_along_axis(listing, (jnp.arange(top)[None, :] + rotation) % top, axis=1)


def portions_of(amount, total, most, slope, full):
    portions = [(1 << 20) // math.isqrt(grade ** slope) + 1 for grade in range(1, amount + 1)]
    largest = most if full else min(most, max(-(-total // amount), total * portions[0] // sum(portions)))
    least = 1 if total - largest >= amount - 1 else 0
    given, rest = [largest] + [least] * (amount - 1), total - largest - least * (amount - 1)
    while rest > 0:
        candidates = [i for i in range(1, amount) if given[i] < largest] or [i for i in range(1, amount) if given[i] < most]
        whole, budget = sum([portions[i] for i in candidates]), rest
        for i in candidates:
            more = min(most - given[i], max(1, budget * portions[i] // whole), rest)
            given[i] = given[i] + more
            rest = rest - more
    return np.array(given)


def gaussian(own_key, shape, spread, bound, pieces=(), held_as=jnp.bfloat16):
    values = jax.random.normal(own_key, shape, jnp.float32) * spread
    if len(pieces) > 0:
        values = shard_levels(own_key, shape, pieces, -0.22, 0.18) * values
    return jnp.clip(values, min=-bound, max=bound).astype(held_as)


def setup_inputs(seed: int = 0) -> dict:
    keys = jax.random.split(jax.random.key(seed), 9)
    tokens = gaussian(keys[0], (TOKENS, D), 1.0, 6.0, ((0, 256),))
    out_grad = gaussian(keys[1], (TOKENS, D), 1.0, 6.0, ((0, 256),))
    expert_ids_keys = jax.random.split(jax.random.fold_in(keys[2], 1), TOKENS // TOK_DEV)
    expert_ids_turns = jax.random.permutation(jax.random.fold_in(keys[2], 3), TOKENS // TOK_DEV)
    expert_ids = jax.vmap(lambda own, number: deal_out(jax.random.fold_in(keys[2], 2), own, number, TOK_DEV, EXPERTS, TOP, CAP, 2))(expert_ids_keys, expert_ids_turns).reshape((TOKENS, TOP))
    gate_weights = jnp.clip(jnp.exp(math.log(1.0) - 2.9957323 * jax.random.uniform(keys[3], (TOKENS, TOP), jnp.float32) ** shard_levels(keys[3], (TOKENS, TOP), ((0, 256),), -0.2, 0.2)), 0.05, 1.0)
    trained = draw_trained(jax.random.fold_in(keys[8], 71), 0)
    w_in = gaussian(keys[5], (EXPERTS, D, 2 * FF), D ** -0.5, 0.125, ((0, 32),))
    w_down = gaussian(keys[6], (EXPERTS, FF, D), FF ** -0.5, 0.21875, ((0, 32),))
    saved = gaussian(keys[7], (N_DP, EXPERTS, N_EXPERT * CAP, 2 * FF), 1.0, 6.0, ((0, 8), (1, 32)))
    return dict(tokens=tokens, out_grad=out_grad, expert_ids=expert_ids, gate_weights=gate_weights, trained=trained, w_in=w_in, w_down=w_down, saved=saved)


def reference(tokens, out_grad, expert_ids, gate_weights, trained, w_in, w_down, saved):
    entry_count = TOK_DEV * TOP
    flat_ids = expert_ids.reshape(DEVICES, entry_count).astype(jnp.int32)
    labels = jnp.arange(EXPERTS, dtype=jnp.int32)
    onehot = (flat_ids[:, :, None] == labels[None, None, :]).astype(jnp.int32)
    slot_rank = jnp.sum(jnp.cumsum(onehot, axis=1) * onehot, axis=2) - 1
    slot_index = (flat_ids * CAP + slot_rank).astype(jnp.int32)
    device_rows = jnp.broadcast_to(jnp.arange(DEVICES, dtype=jnp.int32)[:, None], (DEVICES, entry_count))
    entries = (device_rows * entry_count + jnp.arange(entry_count, dtype=jnp.int32)[None, :]).astype(jnp.int32)
    source = jnp.zeros((DEVICES, EXPERTS * CAP), jnp.int32).at[device_rows, slot_index].set(entries)
    filled = jnp.zeros((DEVICES, EXPERTS * CAP), jnp.float32).at[device_rows, slot_index].set(1.0)
    gate_flat = gate_weights.reshape(-1)

    def one_expert(in_accum, expert):
        start = (expert * CAP).astype(jnp.int32)
        entry_list = lax.dynamic_slice_in_dim(source, start, CAP, 1).reshape(-1)
        live_mask = lax.dynamic_slice_in_dim(filled, start, CAP, 1).reshape(-1)[:, None]
        tok_index = (entry_list // TOP).astype(jnp.int32)
        tok_rows = (tokens[tok_index].astype(jnp.float32) * live_mask).astype(jnp.bfloat16)
        scaled = (gate_flat[entry_list][:, None] * out_grad[tok_index].astype(jnp.float32) * live_mask).astype(jnp.bfloat16)
        saved_rows = lax.dynamic_index_in_dim(saved, expert, 1, keepdims=False)
        saved_rows = saved_rows.reshape(DEVICES * CAP, 2 * FF).astype(jnp.float32)
        gate_pre = saved_rows[:, :FF]
        up_pre = saved_rows[:, FF:]
        weight_in = lax.dynamic_index_in_dim(w_in, expert, 0, keepdims=False)
        weight_down = lax.dynamic_index_in_dim(w_down, expert, 0, keepdims=False)
        hidden_grad = jnp.dot(scaled, weight_down.T, preferred_element_type=jnp.float32)
        sigmoid_gate = jax.nn.sigmoid(gate_pre)
        activated = gate_pre * sigmoid_gate
        pre_grad = jnp.concatenate([hidden_grad * up_pre * sigmoid_gate * (1.0 + gate_pre * (1.0 - sigmoid_gate)), hidden_grad * activated], axis=1).astype(jnp.bfloat16)
        hidden = (activated * up_pre).astype(jnp.bfloat16)
        slot_grads = jnp.dot(pre_grad, weight_in.T, preferred_element_type=jnp.float32).astype(jnp.bfloat16)
        in_accum = in_accum.at[tok_index].add(slot_grads.astype(jnp.float32) * live_mask)
        tok_group = tok_rows.reshape(N_DP, N_EXPERT * CAP, D).astype(jnp.float32)
        scaled_group = scaled.reshape(N_DP, N_EXPERT * CAP, D).astype(jnp.float32)
        pre_group = pre_grad.reshape(N_DP, N_EXPERT * CAP, 2 * FF).astype(jnp.float32)
        hidden_group = hidden.reshape(N_DP, N_EXPERT * CAP, FF).astype(jnp.float32)
        grad_in = jnp.einsum('rsd,rsf->rdf', tok_group, pre_group)
        grad_down = jnp.einsum('rsd,rsf->rdf', scaled_group, hidden_group)
        partial_sums = lax.optimization_barrier(jnp.concatenate([grad_in, grad_down], axis=2).astype(jnp.bfloat16)).astype(jnp.float32)
        trained_flag = jnp.any(trained == expert).astype(jnp.float32)
        weight_block = (jnp.sum(partial_sums, axis=0) * trained_flag).astype(jnp.bfloat16)
        return in_accum, weight_block

    in_accum, weight_grad = lax.scan(one_expert, jnp.zeros((TOKENS, D), jnp.float32), jnp.arange(EXPERTS, dtype=jnp.int32))
    return in_accum.astype(jnp.bfloat16), weight_grad
```

```python
import jax
import jax.numpy as jnp
from jax import lax
from jax.sharding import PartitionSpec as P


def per_device(tokens, out_grad, expert_ids, gate_weights, trained, w_in, w_down, saved):
    groups = lax.axis_size("expert")
    local_count = w_in.shape[0]
    experts = local_count * groups
    tok_count = tokens.shape[0]
    fanout = expert_ids.shape[1]
    slot_total = saved.shape[2]
    capacity = slot_total // groups
    hidden_units = w_down.shape[1]
    f32, bf16 = jnp.float32, jnp.bfloat16

    flat_ids = expert_ids.reshape(-1)
    onehot = (flat_ids[:, None] == jnp.arange(experts, dtype=jnp.int32)[None, :]).astype(jnp.int32)
    slot_rank = jnp.sum(jnp.cumsum(onehot, axis=0) * onehot, axis=1) - 1
    ids4 = flat_ids.reshape(1, 1, tok_count, fanout)
    rank4 = slot_rank.reshape(1, 1, tok_count, fanout)
    sel = (ids4 == jnp.arange(experts, dtype=jnp.int32)[:, None, None, None]) & (
        rank4 == jnp.arange(capacity, dtype=jnp.int32)[None, :, None, None]
    )
    tok_sel = jnp.any(sel, axis=3)
    tok_sel_b = tok_sel.astype(bf16)
    gate_slot = jnp.sum(jnp.where(sel, gate_weights[None, None, :, :], 0.0), axis=(2, 3))

    pick = (((2,), (0,)), ((), ()))
    og_slot = lax.dot_general(tok_sel_b, out_grad, pick, preferred_element_type=f32)
    s_send = (gate_slot[:, :, None] * og_slot).astype(bf16)
    x_send = lax.dot_general(tok_sel_b, tokens, pick, preferred_element_type=f32).astype(bf16)

    s_recv = lax.all_to_all(s_send, "expert", 0, 0, tiled=True)
    x_send, s_recv = lax.optimization_barrier((x_send, s_recv))
    x_recv = lax.all_to_all(x_send, "expert", 0, 0, tiled=True)

    saved3 = saved.reshape(groups, capacity, 2 * hidden_units)
    gate_pre = saved3[:, :, :hidden_units].astype(f32)
    up_pre = saved3[:, :, hidden_units:].astype(f32)
    hidden_grad = lax.dot_general(
        s_recv, w_down[0], (((2,), (1,)), ((), ())), preferred_element_type=f32
    )
    sigmoid_gate = jax.nn.sigmoid(gate_pre)
    activated = gate_pre * sigmoid_gate
    pre_grad = jnp.concatenate(
        [
            hidden_grad * up_pre * sigmoid_gate * (1.0 + gate_pre * (1.0 - sigmoid_gate)),
            hidden_grad * activated,
        ],
        axis=2,
    ).astype(bf16)
    hidden = (activated * up_pre).astype(bf16)
    slot_grads = lax.dot_general(
        pre_grad, w_in[0], (((2,), (1,)), ((), ())), preferred_element_type=f32
    ).astype(bf16)

    trained_flag = jnp.any(trained == lax.axis_index("expert")).astype(f32)
    over_slots = (((0, 1), (0, 1)), ((), ()))
    grad_down = lax.dot_general(s_recv, hidden, over_slots, preferred_element_type=f32)
    down_block = lax.psum_scatter(
        (grad_down * trained_flag).astype(bf16), "dp", scatter_dimension=0, tiled=True
    )

    slot_grads, x_recv = lax.optimization_barrier((slot_grads, x_recv))
    arrived = lax.all_to_all(slot_grads, "expert", 0, 0, tiled=True)

    grad_in = lax.dot_general(x_recv, pre_grad, over_slots, preferred_element_type=f32)
    in_block = lax.psum_scatter(
        (grad_in * trained_flag).astype(bf16), "dp", scatter_dimension=0, tiled=True
    )

    in_grad = lax.dot_general(
        tok_sel_b, arrived, (((0, 1), (0, 1)), ((), ())), preferred_element_type=f32
    ).astype(bf16)
    weight_block = jnp.concatenate([in_block, down_block], axis=1)
    return (in_grad, weight_block[None])


def solution(mesh):
    return jax.shard_map(
        per_device,
        mesh=mesh,
        in_specs=(
            P(("dp", "expert"), None),
            P(("dp", "expert"), None),
            P(("dp", "expert"), None),
            P(("dp", "expert"), None),
            P(),
            P("expert", None, None),
            P("expert", None, None),
            P("dp", "expert", None, None),
        ),
        out_specs=(P(("dp", "expert"), None), P("expert", "dp", None)),
        check_vma=False,
    )
```

```python
import jax
import jax.numpy as jnp
from jax import lax
from jax.experimental import pallas as pl
from jax.experimental.pallas import tpu as pltpu
from jax.sharding import PartitionSpec as P

MESH = pl.DeviceIdType.MESH


def _exchange_kernel(send_ref, recv_ref, send_sems, recv_sems, local_sem):
    n = send_ref.shape[0]
    me = lax.axis_index("expert")
    row = lax.axis_index("dp")
    barrier = pltpu.get_barrier_semaphore()

    def greet(k, carry):
        peer = lax.rem(me + k, n)
        pl.semaphore_signal(barrier, 1, device_id=(row, peer), device_id_type=MESH)
        return carry

    lax.fori_loop(1, n, greet, 0)
    pl.semaphore_wait(barrier, n - 1)
    local = pltpu.make_async_copy(send_ref.at[me], recv_ref.at[me], local_sem)
    local.start()

    def outgoing(peer):
        return pltpu.make_async_remote_copy(
            send_ref.at[peer], recv_ref.at[me], send_sems.at[peer], recv_sems.at[me],
            device_id=(row, peer), device_id_type=MESH,
        )

    def incoming(src):
        return pltpu.make_async_remote_copy(
            send_ref.at[src], recv_ref.at[src], send_sems.at[src], recv_sems.at[src],
            device_id=(row, src), device_id_type=MESH,
        )

    def start(k, carry):
        outgoing(lax.rem(me + k, n)).start()
        return carry

    lax.fori_loop(1, n, start, 0)

    def finish(k, carry):
        outgoing(lax.rem(me + k, n)).wait_send()
        incoming(lax.rem(me + n - k, n)).wait_recv()
        return carry

    lax.fori_loop(1, n, finish, 0)
    local.wait()


def exchange(x, collective):
    n = x.shape[0]
    return pl.pallas_call(
        _exchange_kernel,
        out_shape=jax.ShapeDtypeStruct(x.shape, x.dtype),
        in_specs=[pl.BlockSpec(memory_space=pl.ANY)],
        out_specs=pl.BlockSpec(memory_space=pl.ANY),
        scratch_shapes=[
            pltpu.SemaphoreType.DMA((n,)),
            pltpu.SemaphoreType.DMA((n,)),
            pltpu.SemaphoreType.DMA(()),
        ],
        compiler_params=pltpu.CompilerParams(collective_id=collective, has_side_effects=True),
    )(x)


def per_device(tokens, out_grad, expert_ids, gate_weights, trained, w_in, w_down, saved):
    groups = lax.axis_size("expert")
    local_count = w_in.shape[0]
    experts = local_count * groups
    tok_count = tokens.shape[0]
    fanout = expert_ids.shape[1]
    slot_total = saved.shape[2]
    capacity = slot_total // groups
    hidden_units = w_down.shape[1]
    f32, bf16 = jnp.float32, jnp.bfloat16

    flat_ids = expert_ids.reshape(-1)
    onehot = (flat_ids[:, None] == jnp.arange(experts, dtype=jnp.int32)[None, :]).astype(jnp.int32)
    slot_rank = jnp.sum(jnp.cumsum(onehot, axis=0) * onehot, axis=1) - 1
    ids4 = flat_ids.reshape(1, 1, tok_count, fanout)
    rank4 = slot_rank.reshape(1, 1, tok_count, fanout)
    sel = (ids4 == jnp.arange(experts, dtype=jnp.int32)[:, None, None, None]) & (
        rank4 == jnp.arange(capacity, dtype=jnp.int32)[None, :, None, None]
    )
    tok_sel = jnp.any(sel, axis=3)
    tok_sel_b = tok_sel.astype(bf16)
    gate_slot = jnp.sum(jnp.where(sel, gate_weights[None, None, :, :], 0.0), axis=(2, 3))

    pick = (((2,), (0,)), ((), ()))
    og_slot = lax.dot_general(tok_sel_b, out_grad, pick, preferred_element_type=f32)
    s_send = (gate_slot[:, :, None] * og_slot).astype(bf16)
    x_send = lax.dot_general(tok_sel_b, tokens, pick, preferred_element_type=f32).astype(bf16)

    s_recv = exchange(s_send, 0)

    saved3 = saved.reshape(groups, capacity, 2 * hidden_units)
    gate_pre = saved3[:, :, :hidden_units].astype(f32)
    up_pre = saved3[:, :, hidden_units:].astype(f32)
    hidden_grad = lax.dot_general(
        s_recv, w_down[0], (((2,), (1,)), ((), ())), preferred_element_type=f32
    )
    sigmoid_gate = jax.nn.sigmoid(gate_pre)
    activated = gate_pre * sigmoid_gate
    pre_grad = jnp.concatenate(
        [
            hidden_grad * up_pre * sigmoid_gate * (1.0 + gate_pre * (1.0 - sigmoid_gate)),
            hidden_grad * activated,
        ],
        axis=2,
    ).astype(bf16)
    hidden = (activated * up_pre).astype(bf16)
    slot_grads = lax.dot_general(
        pre_grad, w_in[0], (((2,), (1,)), ((), ())), preferred_element_type=f32
    ).astype(bf16)

    trained_flag = jnp.any(trained == lax.axis_index("expert")).astype(f32)
    over_slots = (((0, 1), (0, 1)), ((), ()))
    grad_down = lax.dot_general(s_recv, hidden, over_slots, preferred_element_type=f32)
    down_part = (grad_down * trained_flag).astype(bf16)
    x_send, down_part = lax.optimization_barrier((x_send, down_part))
    down_block = lax.psum_scatter(down_part, "dp", scatter_dimension=0, tiled=True)
    x_recv = exchange(x_send, 1)

    slot_grads, x_recv = lax.optimization_barrier((slot_grads, x_recv))
    arrived = exchange(slot_grads, 2)

    grad_in = lax.dot_general(x_recv, pre_grad, over_slots, preferred_element_type=f32)
    in_block = lax.psum_scatter(
        (grad_in * trained_flag).astype(bf16), "dp", scatter_dimension=0, tiled=True
    )

    in_grad = lax.dot_general(
        tok_sel_b, arrived, (((0, 1), (0, 1)), ((), ())), preferred_element_type=f32
    ).astype(bf16)
    weight_block = jnp.concatenate([in_block, down_block], axis=1)
    return (in_grad, weight_block[None])


def solution(mesh):
    return jax.shard_map(
        per_device,
        mesh=mesh,
        in_specs=(
            P(("dp", "expert"), None),
            P(("dp", "expert"), None),
            P(("dp", "expert"), None),
            P(("dp", "expert"), None),
            P(),
            P("expert", None, None),
            P("expert", None, None),
            P("dp", "expert", None, None),
        ),
        out_specs=(P(("dp", "expert"), None), P("expert", "dp", None)),
        check_vma=False,
    )
```

```python
import jax
import jax.numpy as jnp
from jax import lax
from jax.experimental.layout import Layout, with_layout_constraint
from jax.sharding import PartitionSpec as P


def row_major(x):
    return with_layout_constraint(x, Layout(major_to_minor=tuple(range(x.ndim))))


def col_major(x):
    return with_layout_constraint(x, Layout(major_to_minor=(1, 0)))


def per_device(tokens, out_grad, expert_ids, gate_weights, trained, w_in, w_down, saved):
    groups = lax.axis_size("expert")
    local_count = w_in.shape[0]
    experts = local_count * groups
    tok_count = tokens.shape[0]
    fanout = expert_ids.shape[1]
    slot_total = saved.shape[2]
    capacity = slot_total // groups
    hidden_units = w_down.shape[1]
    f32, bf16 = jnp.float32, jnp.bfloat16

    flat_ids = expert_ids.reshape(-1)
    onehot = (flat_ids[:, None] == jnp.arange(experts, dtype=jnp.int32)[None, :]).astype(jnp.int32)
    slot_rank = jnp.sum(jnp.cumsum(onehot, axis=0) * onehot, axis=1) - 1
    ids4 = flat_ids.reshape(1, 1, tok_count, fanout)
    rank4 = slot_rank.reshape(1, 1, tok_count, fanout)
    sel = (ids4 == jnp.arange(experts, dtype=jnp.int32)[:, None, None, None]) & (
        rank4 == jnp.arange(capacity, dtype=jnp.int32)[None, :, None, None]
    )
    tok_sel = jnp.any(sel, axis=3)
    tok_sel_b = tok_sel.astype(bf16)
    gate_slot = jnp.sum(jnp.where(sel, gate_weights[None, None, :, :], 0.0), axis=(2, 3))

    pick = (((2,), (0,)), ((), ()))
    og_slot = lax.dot_general(tok_sel_b, out_grad, pick, preferred_element_type=f32)
    s_send = (gate_slot[:, :, None] * og_slot).astype(bf16)
    x_send = lax.dot_general(tok_sel_b, tokens, pick, preferred_element_type=f32).astype(bf16)

    saved3 = saved.reshape(groups, capacity, 2 * hidden_units)
    gate_pre = saved3[:, :, :hidden_units].astype(f32)
    up_pre = saved3[:, :, hidden_units:].astype(f32)
    sigmoid_gate = jax.nn.sigmoid(gate_pre)
    activated = gate_pre * sigmoid_gate
    hidden = (activated * up_pre).astype(bf16)

    s_recv = lax.all_to_all(row_major(s_send), "expert", 0, 0, tiled=True)
    x_send, s_recv, hidden = lax.optimization_barrier((x_send, s_recv, hidden))
    x_recv = lax.all_to_all(row_major(x_send), "expert", 0, 0, tiled=True)

    trained_flag = jnp.any(trained == lax.axis_index("expert")).astype(f32)
    over_slots = (((0, 1), (0, 1)), ((), ()))
    grad_down = lax.dot_general(s_recv, hidden, over_slots, preferred_element_type=f32)
    down_part = col_major((grad_down * trained_flag).astype(bf16))
    down_part, s_recv = lax.optimization_barrier((down_part, s_recv))
    down_block = lax.psum_scatter(down_part, "dp", scatter_dimension=0, tiled=True)

    hidden_grad = lax.dot_general(
        s_recv, w_down[0], (((2,), (1,)), ((), ())), preferred_element_type=f32
    )
    pre_grad = jnp.concatenate(
        [
            hidden_grad * up_pre * sigmoid_gate * (1.0 + gate_pre * (1.0 - sigmoid_gate)),
            hidden_grad * activated,
        ],
        axis=2,
    ).astype(bf16)
    slot_grads = lax.dot_general(
        pre_grad, w_in[0], (((2,), (1,)), ((), ())), preferred_element_type=f32
    ).astype(bf16)

    slot_grads, x_recv = lax.optimization_barrier((slot_grads, x_recv))
    arrived = lax.all_to_all(row_major(slot_grads), "expert", 0, 0, tiled=True)

    grad_in = lax.dot_general(x_recv, pre_grad, over_slots, preferred_element_type=f32)
    in_part = col_major((grad_in * trained_flag).astype(bf16))
    in_block = lax.psum_scatter(in_part, "dp", scatter_dimension=0, tiled=True)

    in_grad = lax.dot_general(
        tok_sel_b, arrived, (((0, 1), (0, 1)), ((), ())), preferred_element_type=f32
    ).astype(bf16)
    weight_block = jnp.concatenate([in_block, down_block], axis=1)
    return (in_grad, weight_block[None])


def solution(mesh):
    return jax.shard_map(
        per_device,
        mesh=mesh,
        in_specs=(
            P(("dp", "expert"), None),
            P(("dp", "expert"), None),
            P(("dp", "expert"), None),
            P(("dp", "expert"), None),
            P(),
            P("expert", None, None),
            P("expert", None, None),
            P("dp", "expert", None, None),
        ),
        out_specs=(P(("dp", "expert"), None), P("expert", "dp", None)),
        check_vma=False,
    )
```

```python
import jax
import jax.numpy as jnp
from jax import lax
from jax.experimental.layout import Layout, with_layout_constraint
from jax.sharding import PartitionSpec as P


def row_major(x):
    return with_layout_constraint(x, Layout(major_to_minor=tuple(range(x.ndim))))


def col_major(x):
    return with_layout_constraint(x, Layout(major_to_minor=(1, 0)))


def per_device(tokens, out_grad, expert_ids, gate_weights, trained, w_in, w_down, saved):
    groups = lax.axis_size("expert")
    local_count = w_in.shape[0]
    experts = local_count * groups
    tok_count = tokens.shape[0]
    fanout = expert_ids.shape[1]
    slot_total = saved.shape[2]
    capacity = slot_total // groups
    hidden_units = w_down.shape[1]
    f32, bf16 = jnp.float32, jnp.bfloat16

    flat_ids = expert_ids.reshape(-1)
    onehot = (flat_ids[:, None] == jnp.arange(experts, dtype=jnp.int32)[None, :]).astype(jnp.int32)
    slot_rank = jnp.sum(jnp.cumsum(onehot, axis=0) * onehot, axis=1) - 1
    ids4 = flat_ids.reshape(1, 1, tok_count, fanout)
    rank4 = slot_rank.reshape(1, 1, tok_count, fanout)
    sel = (ids4 == jnp.arange(experts, dtype=jnp.int32)[:, None, None, None]) & (
        rank4 == jnp.arange(capacity, dtype=jnp.int32)[None, :, None, None]
    )
    tok_sel = jnp.any(sel, axis=3)
    tok_sel_b = tok_sel.astype(bf16)
    gate_slot = jnp.sum(jnp.where(sel, gate_weights[None, None, :, :], 0.0), axis=(2, 3))
    slot_tok = jnp.sum(jnp.where(tok_sel, jnp.arange(tok_count, dtype=jnp.int32), 0), axis=2)
    filled = jnp.any(tok_sel, axis=2).reshape(-1)

    lanes = 128
    rows = tokens.shape[1] // lanes
    flat = (groups, capacity * rows, lanes)
    tok3 = tokens.reshape(tok_count, rows, lanes)
    og3 = out_grad.reshape(tok_count, rows, lanes)
    slot_rows = slot_tok.reshape(-1)
    x_send = jnp.where(filled[:, None, None], tok3[slot_rows], jnp.zeros((), bf16)).reshape(flat)
    s_send = (gate_slot.reshape(-1)[:, None, None] * og3[slot_rows].astype(f32)).astype(bf16)
    s_send = s_send.reshape(flat)

    saved3 = saved.reshape(groups, capacity, 2 * hidden_units)
    gate_pre = saved3[:, :, :hidden_units].astype(f32)
    up_pre = saved3[:, :, hidden_units:].astype(f32)
    sigmoid_gate = jax.nn.sigmoid(gate_pre)
    activated = gate_pre * sigmoid_gate
    hidden = (activated * up_pre).astype(bf16)

    s_recv = lax.all_to_all(row_major(s_send), "expert", 0, 0, tiled=True)
    s_recv = s_recv.reshape(groups, capacity, rows * lanes)
    x_send, s_recv, hidden = lax.optimization_barrier((x_send, s_recv, hidden))
    x_recv = lax.all_to_all(row_major(x_send), "expert", 0, 0, tiled=True)
    x_recv = x_recv.reshape(groups, capacity, rows * lanes)

    trained_flag = jnp.any(trained == lax.axis_index("expert")).astype(f32)
    over_slots = (((0, 1), (0, 1)), ((), ()))
    grad_down = lax.dot_general(s_recv, hidden, over_slots, preferred_element_type=f32)
    down_part = col_major((grad_down * trained_flag).astype(bf16))
    down_part, s_recv = lax.optimization_barrier((down_part, s_recv))
    down_block = lax.psum_scatter(down_part, "dp", scatter_dimension=0, tiled=True)

    hidden_grad = lax.dot_general(
        s_recv, w_down[0], (((2,), (1,)), ((), ())), preferred_element_type=f32
    )
    pre_grad = jnp.concatenate(
        [
            hidden_grad * up_pre * sigmoid_gate * (1.0 + gate_pre * (1.0 - sigmoid_gate)),
            hidden_grad * activated,
        ],
        axis=2,
    ).astype(bf16)
    slot_grads = lax.dot_general(
        pre_grad, w_in[0], (((2,), (1,)), ((), ())), preferred_element_type=f32
    ).astype(bf16)

    slot_grads, x_recv = lax.optimization_barrier((slot_grads, x_recv))
    slot_grads = slot_grads.reshape(flat)
    arrived = lax.all_to_all(row_major(slot_grads), "expert", 0, 0, tiled=True)

    grad_in = lax.dot_general(x_recv, pre_grad, over_slots, preferred_element_type=f32)
    in_part = col_major((grad_in * trained_flag).astype(bf16))
    in_block = lax.psum_scatter(in_part, "dp", scatter_dimension=0, tiled=True)

    slot_index = flat_ids * capacity + slot_rank
    picked = arrived.reshape(groups * capacity, rows, lanes)[slot_index]
    in_grad = jnp.sum(picked.reshape(tok_count, fanout, rows, lanes).astype(f32), axis=1)
    in_grad = in_grad.astype(bf16).reshape(tok_count, rows * lanes)
    weight_block = jnp.concatenate([in_block, down_block], axis=1)
    return (in_grad, weight_block[None])


def solution(mesh):
    return jax.shard_map(
        per_device,
        mesh=mesh,
        in_specs=(
            P(("dp", "expert"), None),
            P(("dp", "expert"), None),
            P(("dp", "expert"), None),
            P(("dp", "expert"), None),
            P(),
            P("expert", None, None),
            P("expert", None, None),
            P("dp", "expert", None, None),
        ),
        out_specs=(P(("dp", "expert"), None), P("expert", "dp", None)),
        check_vma=False,
    )
```

```python
import jax
import jax.numpy as jnp
from jax import lax
from jax.experimental.layout import Layout, with_layout_constraint
from jax.sharding import PartitionSpec as P


def row_major(x):
    return with_layout_constraint(x, Layout(major_to_minor=tuple(range(x.ndim))))


def col_major(x):
    return with_layout_constraint(x, Layout(major_to_minor=(1, 0)))


def per_device(tokens, out_grad, expert_ids, gate_weights, trained, w_in, w_down, saved):
    groups = lax.axis_size("expert")
    local_count = w_in.shape[0]
    experts = local_count * groups
    tok_count = tokens.shape[0]
    fanout = expert_ids.shape[1]
    slot_total = saved.shape[2]
    capacity = slot_total // groups
    hidden_units = w_down.shape[1]
    f32, bf16 = jnp.float32, jnp.bfloat16

    flat_ids = expert_ids.reshape(-1)
    onehot = (flat_ids[:, None] == jnp.arange(experts, dtype=jnp.int32)[None, :]).astype(jnp.int32)
    slot_rank = jnp.sum(jnp.cumsum(onehot, axis=0) * onehot, axis=1) - 1
    ids4 = flat_ids.reshape(1, 1, tok_count, fanout)
    rank4 = slot_rank.reshape(1, 1, tok_count, fanout)
    sel = (ids4 == jnp.arange(experts, dtype=jnp.int32)[:, None, None, None]) & (
        rank4 == jnp.arange(capacity, dtype=jnp.int32)[None, :, None, None]
    )
    tok_sel = jnp.any(sel, axis=3)
    tok_sel_b = tok_sel.astype(bf16)
    gate_slot = jnp.sum(jnp.where(sel, gate_weights[None, None, :, :], 0.0), axis=(2, 3))

    pick = (((2,), (0,)), ((), ()))
    og_slot = lax.dot_general(tok_sel_b, out_grad, pick, preferred_element_type=f32)
    s_send = (gate_slot[:, :, None] * og_slot).astype(bf16)
    lanes = 128
    rows = tokens.shape[1] // lanes
    slot_tok = jnp.sum(jnp.where(tok_sel, jnp.arange(tok_count, dtype=jnp.int32), 0), axis=2)
    filled = jnp.any(tok_sel, axis=2).reshape(-1)
    tok3 = tokens.reshape(tok_count, rows, lanes)
    x_send = jnp.where(filled[:, None, None], tok3[slot_tok.reshape(-1)], jnp.zeros((), bf16))
    x_send = x_send.reshape(groups, capacity * rows, lanes)

    saved3 = saved.reshape(groups, capacity, 2 * hidden_units)
    gate_pre = saved3[:, :, :hidden_units].astype(f32)
    up_pre = saved3[:, :, hidden_units:].astype(f32)
    sigmoid_gate = jax.nn.sigmoid(gate_pre)
    activated = gate_pre * sigmoid_gate
    hidden = (activated * up_pre).astype(bf16)

    s_recv = lax.all_to_all(row_major(s_send), "expert", 0, 0, tiled=True)
    x_send, s_recv, hidden = lax.optimization_barrier((x_send, s_recv, hidden))
    x_recv = lax.all_to_all(row_major(x_send), "expert", 0, 0, tiled=True)

    trained_flag = jnp.any(trained == lax.axis_index("expert")).astype(f32)
    over_slots = (((0, 1), (0, 1)), ((), ()))
    grad_down = lax.dot_general(s_recv, hidden, over_slots, preferred_element_type=f32)
    down_part = col_major((grad_down * trained_flag).astype(bf16))
    down_part, s_recv = lax.optimization_barrier((down_part, s_recv))
    down_block = lax.psum_scatter(down_part, "dp", scatter_dimension=0, tiled=True)

    hidden_grad = lax.dot_general(
        s_recv, w_down[0], (((2,), (1,)), ((), ())), preferred_element_type=f32
    )
    pre_grad = jnp.concatenate(
        [
            hidden_grad * up_pre * sigmoid_gate * (1.0 + gate_pre * (1.0 - sigmoid_gate)),
            hidden_grad * activated,
        ],
        axis=2,
    ).astype(bf16)
    slot_grads = lax.dot_general(
        pre_grad, w_in[0], (((2,), (1,)), ((), ())), preferred_element_type=f32
    ).astype(bf16)

    slot_grads, x_recv = lax.optimization_barrier((slot_grads, x_recv))
    arrived = lax.all_to_all(row_major(slot_grads), "expert", 0, 0, tiled=True)

    x_rows = x_recv.reshape(groups * capacity, rows, lanes)
    pre_rows = pre_grad.reshape(groups * capacity, 2 * hidden_units)
    grad_in = lax.dot_general(x_rows, pre_rows, (((0,), (0,)), ((), ())), preferred_element_type=f32)
    in_part = (grad_in.reshape(rows * lanes, 2 * hidden_units) * trained_flag).astype(bf16)
    in_block = lax.psum_scatter(in_part, "dp", scatter_dimension=0, tiled=True)

    in_grad = lax.dot_general(
        tok_sel_b, arrived, (((0, 1), (0, 1)), ((), ())), preferred_element_type=f32
    ).astype(bf16)
    weight_block = jnp.concatenate([in_block, down_block], axis=1)
    return (in_grad, weight_block[None])


def solution(mesh):
    return jax.shard_map(
        per_device,
        mesh=mesh,
        in_specs=(
            P(("dp", "expert"), None),
            P(("dp", "expert"), None),
            P(("dp", "expert"), None),
            P(("dp", "expert"), None),
            P(),
            P("expert", None, None),
            P("expert", None, None),
            P("dp", "expert", None, None),
        ),
        out_specs=(P(("dp", "expert"), None), P("expert", "dp", None)),
        check_vma=False,
    )
```

```python
import jax
import jax.numpy as jnp
from jax import lax
from jax.experimental.layout import Layout, with_layout_constraint
from jax.sharding import PartitionSpec as P


def row_major(x):
    return with_layout_constraint(x, Layout(major_to_minor=tuple(range(x.ndim))))


def col_major(x):
    return with_layout_constraint(x, Layout(major_to_minor=(1, 0)))


def per_device(tokens, out_grad, expert_ids, gate_weights, trained, w_in, w_down, saved):
    groups = lax.axis_size("expert")
    local_count = w_in.shape[0]
    experts = local_count * groups
    tok_count = tokens.shape[0]
    fanout = expert_ids.shape[1]
    slot_total = saved.shape[2]
    capacity = slot_total // groups
    hidden_units = w_down.shape[1]
    f32, bf16 = jnp.float32, jnp.bfloat16

    flat_ids = expert_ids.reshape(-1)
    onehot = (flat_ids[:, None] == jnp.arange(experts, dtype=jnp.int32)[None, :]).astype(jnp.int32)
    slot_rank = jnp.sum(jnp.cumsum(onehot, axis=0) * onehot, axis=1) - 1
    ids4 = flat_ids.reshape(1, 1, tok_count, fanout)
    rank4 = slot_rank.reshape(1, 1, tok_count, fanout)
    sel = (ids4 == jnp.arange(experts, dtype=jnp.int32)[:, None, None, None]) & (
        rank4 == jnp.arange(capacity, dtype=jnp.int32)[None, :, None, None]
    )
    tok_sel = jnp.any(sel, axis=3)
    tok_sel_b = tok_sel.astype(bf16)
    gate_slot = jnp.sum(jnp.where(sel, gate_weights[None, None, :, :], 0.0), axis=(2, 3))

    lanes = 128
    rows = tokens.shape[1] // lanes
    flat = (groups, capacity * rows, lanes)
    slot_tok = jnp.sum(jnp.where(tok_sel, jnp.arange(tok_count, dtype=jnp.int32), 0), axis=2)
    filled = jnp.any(tok_sel, axis=2).reshape(-1)
    slot_rows = slot_tok.reshape(-1)
    og_send = out_grad.reshape(tok_count, rows, lanes)[slot_rows].reshape(flat)
    tok3 = tokens.reshape(tok_count, rows, lanes)
    x_send = jnp.where(filled[:, None, None], tok3[slot_rows], jnp.zeros((), bf16)).reshape(flat)

    saved3 = saved.reshape(groups, capacity, 2 * hidden_units)
    gate_pre = saved3[:, :, :hidden_units].astype(f32)
    up_pre = saved3[:, :, hidden_units:].astype(f32)
    sigmoid_gate = jax.nn.sigmoid(gate_pre)
    activated = gate_pre * sigmoid_gate
    hidden = (activated * up_pre).astype(bf16)

    og_recv = lax.all_to_all(row_major(og_send), "expert", 0, 0, tiled=True)
    gate_recv = lax.all_to_all(gate_slot, "expert", 0, 0, tiled=True)
    x_send, og_recv, gate_recv, hidden = lax.optimization_barrier(
        (x_send, og_recv, gate_recv, hidden)
    )
    slot_count = groups * capacity
    s_rows = (
        gate_recv.reshape(slot_count, 1, 1) * og_recv.reshape(slot_count, rows, lanes).astype(f32)
    ).astype(bf16)
    x_recv = lax.all_to_all(row_major(x_send), "expert", 0, 0, tiled=True)

    trained_flag = jnp.any(trained == lax.axis_index("expert")).astype(f32)
    over_slots = (((0, 1), (0, 1)), ((), ()))
    grad_down = lax.dot_general(
        s_rows, hidden.reshape(slot_count, hidden_units), (((0,), (0,)), ((), ())),
        preferred_element_type=f32,
    )
    down_part = (grad_down.reshape(rows * lanes, hidden_units) * trained_flag).astype(bf16)
    down_part, s_rows = lax.optimization_barrier((down_part, s_rows))
    s_recv = s_rows.reshape(groups, capacity, rows * lanes)
    down_block = lax.psum_scatter(down_part, "dp", scatter_dimension=0, tiled=True)

    hidden_grad = lax.dot_general(
        s_recv, w_down[0], (((2,), (1,)), ((), ())), preferred_element_type=f32
    )
    pre_grad = jnp.concatenate(
        [
            hidden_grad * up_pre * sigmoid_gate * (1.0 + gate_pre * (1.0 - sigmoid_gate)),
            hidden_grad * activated,
        ],
        axis=2,
    ).astype(bf16)
    slot_grads = lax.dot_general(
        pre_grad, w_in[0], (((2,), (1,)), ((), ())), preferred_element_type=f32
    ).astype(bf16)

    slot_grads, x_recv = lax.optimization_barrier((slot_grads, x_recv))
    arrived = lax.all_to_all(row_major(slot_grads), "expert", 0, 0, tiled=True)

    x_rows = x_recv.reshape(slot_count, rows, lanes)
    pre_rows = pre_grad.reshape(slot_count, 2 * hidden_units)
    grad_in = lax.dot_general(x_rows, pre_rows, (((0,), (0,)), ((), ())), preferred_element_type=f32)
    in_part = (grad_in.reshape(rows * lanes, 2 * hidden_units) * trained_flag).astype(bf16)
    in_block = lax.psum_scatter(in_part, "dp", scatter_dimension=0, tiled=True)

    in_grad = lax.dot_general(
        tok_sel_b, arrived, (((0, 1), (0, 1)), ((), ())), preferred_element_type=f32
    ).astype(bf16)
    weight_block = jnp.concatenate([in_block, down_block], axis=1)
    return (in_grad, weight_block[None])


def solution(mesh):
    return jax.shard_map(
        per_device,
        mesh=mesh,
        in_specs=(
            P(("dp", "expert"), None),
            P(("dp", "expert"), None),
            P(("dp", "expert"), None),
            P(("dp", "expert"), None),
            P(),
            P("expert", None, None),
            P("expert", None, None),
            P("dp", "expert", None, None),
        ),
        out_specs=(P(("dp", "expert"), None), P("expert", "dp", None)),
        check_vma=False,
    )
```

```python
import jax
import jax.numpy as jnp
from jax import lax
from jax.experimental.layout import Layout, with_layout_constraint
from jax.sharding import PartitionSpec as P


def row_major(x):
    return with_layout_constraint(x, Layout(major_to_minor=tuple(range(x.ndim))))


def col_major(x):
    return with_layout_constraint(x, Layout(major_to_minor=(1, 0)))


def per_device(tokens, out_grad, expert_ids, gate_weights, trained, w_in, w_down, saved):
    groups = lax.axis_size("expert")
    local_count = w_in.shape[0]
    experts = local_count * groups
    tok_count = tokens.shape[0]
    fanout = expert_ids.shape[1]
    slot_total = saved.shape[2]
    capacity = slot_total // groups
    hidden_units = w_down.shape[1]
    f32, bf16 = jnp.float32, jnp.bfloat16

    flat_ids = expert_ids.reshape(-1)
    onehot = (flat_ids[:, None] == jnp.arange(experts, dtype=jnp.int32)[None, :]).astype(jnp.int32)
    slot_rank = jnp.sum(jnp.cumsum(onehot, axis=0) * onehot, axis=1) - 1
    ids4 = flat_ids.reshape(1, 1, tok_count, fanout)
    rank4 = slot_rank.reshape(1, 1, tok_count, fanout)
    sel = (ids4 == jnp.arange(experts, dtype=jnp.int32)[:, None, None, None]) & (
        rank4 == jnp.arange(capacity, dtype=jnp.int32)[None, :, None, None]
    )
    tok_sel = jnp.any(sel, axis=3)
    tok_sel_b = tok_sel.astype(bf16)
    gate_slot = jnp.sum(jnp.where(sel, gate_weights[None, None, :, :], 0.0), axis=(2, 3))

    lanes = 128
    rows = tokens.shape[1] // lanes
    flat = (groups, capacity * rows, lanes)
    slot_count = groups * capacity
    slot_tok = jnp.sum(jnp.where(tok_sel, jnp.arange(tok_count, dtype=jnp.int32), 0), axis=2)
    filled = jnp.any(tok_sel, axis=2).reshape(-1)
    slot_rows = slot_tok.reshape(-1)
    og3 = out_grad.reshape(tok_count, rows, lanes)
    s_send = (gate_slot.reshape(-1)[:, None, None] * og3[slot_rows].astype(f32)).astype(bf16)
    s_send = s_send.reshape(flat)
    tok3 = tokens.reshape(tok_count, rows, lanes)
    x_send = jnp.where(filled[:, None, None], tok3[slot_rows], jnp.zeros((), bf16)).reshape(flat)

    saved_rows = saved.reshape(slot_count, 2 * hidden_units)
    gate_rows = saved_rows[:, :hidden_units].astype(f32)
    activated_rows = gate_rows * jax.nn.sigmoid(gate_rows)
    hidden_rows = (activated_rows * saved_rows[:, hidden_units:].astype(f32)).astype(bf16)

    saved3 = saved.reshape(groups, capacity, 2 * hidden_units)
    gate_pre = saved3[:, :, :hidden_units].astype(f32)
    up_pre = saved3[:, :, hidden_units:].astype(f32)
    sigmoid_gate = jax.nn.sigmoid(gate_pre)
    activated = gate_pre * sigmoid_gate

    s_recv = lax.all_to_all(row_major(s_send), "expert", 0, 0, tiled=True)
    x_send, s_recv, hidden_rows = lax.optimization_barrier((x_send, s_recv, hidden_rows))
    x_recv = lax.all_to_all(row_major(x_send), "expert", 0, 0, tiled=True)

    trained_flag = jnp.any(trained == lax.axis_index("expert")).astype(f32)
    over_slots = (((0, 1), (0, 1)), ((), ()))
    grad_down = lax.dot_general(
        s_recv.reshape(slot_count, rows, lanes), hidden_rows, (((0,), (0,)), ((), ())),
        preferred_element_type=f32,
    )
    down_part = (grad_down.reshape(rows * lanes, hidden_units) * trained_flag).astype(bf16)
    down_part, s_recv = lax.optimization_barrier((down_part, s_recv))
    s_recv = s_recv.reshape(groups, capacity, rows * lanes)
    down_block = lax.psum_scatter(down_part, "dp", scatter_dimension=0, tiled=True)

    hidden_grad = lax.dot_general(
        s_recv, w_down[0], (((2,), (1,)), ((), ())), preferred_element_type=f32
    )
    pre_grad = jnp.concatenate(
        [
            hidden_grad * up_pre * sigmoid_gate * (1.0 + gate_pre * (1.0 - sigmoid_gate)),
            hidden_grad * activated,
        ],
        axis=2,
    ).astype(bf16)
    slot_grads = lax.dot_general(
        pre_grad, w_in[0], (((2,), (1,)), ((), ())), preferred_element_type=f32
    ).astype(bf16)

    slot_grads, x_recv = lax.optimization_barrier((slot_grads, x_recv))
    arrived = lax.all_to_all(row_major(slot_grads), "expert", 0, 0, tiled=True)

    x_rows = x_recv.reshape(slot_count, rows, lanes)
    pre_rows = pre_grad.reshape(slot_count, 2 * hidden_units)
    grad_in = lax.dot_general(x_rows, pre_rows, (((0,), (0,)), ((), ())), preferred_element_type=f32)
    in_part = (grad_in.reshape(rows * lanes, 2 * hidden_units) * trained_flag).astype(bf16)
    in_block = lax.psum_scatter(in_part, "dp", scatter_dimension=0, tiled=True)

    in_grad = lax.dot_general(
        tok_sel_b, arrived, (((0, 1), (0, 1)), ((), ())), preferred_element_type=f32
    ).astype(bf16)
    weight_block = jnp.concatenate([in_block, down_block], axis=1)
    return (in_grad, weight_block[None])


def solution(mesh):
    return jax.shard_map(
        per_device,
        mesh=mesh,
        in_specs=(
            P(("dp", "expert"), None),
            P(("dp", "expert"), None),
            P(("dp", "expert"), None),
            P(("dp", "expert"), None),
            P(),
            P("expert", None, None),
            P("expert", None, None),
            P("dp", "expert", None, None),
        ),
        out_specs=(P(("dp", "expert"), None), P("expert", "dp", None)),
        check_vma=False,
    )
```

```python
import jax
import jax.numpy as jnp
from jax import lax
from jax.experimental.layout import Layout, with_layout_constraint
from jax.sharding import PartitionSpec as P


def row_major(x):
    return with_layout_constraint(x, Layout(major_to_minor=tuple(range(x.ndim))))


def col_major(x):
    return with_layout_constraint(x, Layout(major_to_minor=(1, 0)))


def per_device(tokens, out_grad, expert_ids, gate_weights, trained, w_in, w_down, saved):
    groups = lax.axis_size("expert")
    local_count = w_in.shape[0]
    experts = local_count * groups
    tok_count = tokens.shape[0]
    fanout = expert_ids.shape[1]
    slot_total = saved.shape[2]
    capacity = slot_total // groups
    hidden_units = w_down.shape[1]
    f32, bf16 = jnp.float32, jnp.bfloat16

    flat_ids = expert_ids.reshape(-1)
    entries = flat_ids.shape[0]
    onehot = (flat_ids[:, None] == jnp.arange(experts, dtype=jnp.int32)[None, :]).astype(bf16)
    order = jnp.arange(entries, dtype=jnp.int32)
    earlier = (order[:, None] > order[None, :]).astype(bf16)
    before = lax.dot_general(earlier, onehot, (((1,), (0,)), ((), ())), preferred_element_type=f32)
    slot_rank = jnp.sum(before * onehot.astype(f32), axis=1).astype(jnp.int32)
    ids4 = flat_ids.reshape(1, 1, tok_count, fanout)
    rank4 = slot_rank.reshape(1, 1, tok_count, fanout)
    sel = (ids4 == jnp.arange(experts, dtype=jnp.int32)[:, None, None, None]) & (
        rank4 == jnp.arange(capacity, dtype=jnp.int32)[None, :, None, None]
    )
    tok_sel = jnp.any(sel, axis=3)
    tok_sel_b = tok_sel.astype(bf16)
    gate_slot = jnp.sum(jnp.where(sel, gate_weights[None, None, :, :], 0.0), axis=(2, 3))

    pick = (((2,), (0,)), ((), ()))
    og_slot = lax.dot_general(tok_sel_b, out_grad, pick, preferred_element_type=f32)
    s_send = (gate_slot[:, :, None] * og_slot).astype(bf16)
    lanes = 128
    rows = tokens.shape[1] // lanes
    slot_tok = jnp.sum(jnp.where(tok_sel, jnp.arange(tok_count, dtype=jnp.int32), 0), axis=2)
    filled = jnp.any(tok_sel, axis=2).reshape(-1)
    tok3 = tokens.reshape(tok_count, rows, lanes)
    x_send = jnp.where(filled[:, None, None], tok3[slot_tok.reshape(-1)], jnp.zeros((), bf16))
    x_send = x_send.reshape(groups, capacity * rows, lanes)

    saved3 = saved.reshape(groups, capacity, 2 * hidden_units)
    gate_pre = saved3[:, :, :hidden_units].astype(f32)
    up_pre = saved3[:, :, hidden_units:].astype(f32)
    sigmoid_gate = jax.nn.sigmoid(gate_pre)
    activated = gate_pre * sigmoid_gate
    hidden = (activated * up_pre).astype(bf16)

    s_recv = lax.all_to_all(row_major(s_send), "expert", 0, 0, tiled=True)
    x_send, s_recv, hidden = lax.optimization_barrier((x_send, s_recv, hidden))
    x_recv = lax.all_to_all(row_major(x_send), "expert", 0, 0, tiled=True)

    trained_flag = jnp.any(trained == lax.axis_index("expert")).astype(f32)
    over_slots = (((0, 1), (0, 1)), ((), ()))
    grad_down = lax.dot_general(s_recv, hidden, over_slots, preferred_element_type=f32)
    down_part = col_major((grad_down * trained_flag).astype(bf16))
    down_part, s_recv = lax.optimization_barrier((down_part, s_recv))
    down_block = lax.psum_scatter(down_part, "dp", scatter_dimension=0, tiled=True)

    hidden_grad = lax.dot_general(
        s_recv, w_down[0], (((2,), (1,)), ((), ())), preferred_element_type=f32
    )
    pre_grad = jnp.concatenate(
        [
            hidden_grad * up_pre * sigmoid_gate * (1.0 + gate_pre * (1.0 - sigmoid_gate)),
            hidden_grad * activated,
        ],
        axis=2,
    ).astype(bf16)
    slot_grads = lax.dot_general(
        pre_grad, w_in[0], (((2,), (1,)), ((), ())), preferred_element_type=f32
    ).astype(bf16)

    slot_grads, x_recv = lax.optimization_barrier((slot_grads, x_recv))
    arrived = lax.all_to_all(row_major(slot_grads), "expert", 0, 0, tiled=True)

    x_rows = x_recv.reshape(groups * capacity, rows, lanes)
    pre_rows = pre_grad.reshape(groups * capacity, 2 * hidden_units)
    grad_in = lax.dot_general(x_rows, pre_rows, (((0,), (0,)), ((), ())), preferred_element_type=f32)
    in_part = (grad_in.reshape(rows * lanes, 2 * hidden_units) * trained_flag).astype(bf16)
    in_block = lax.psum_scatter(in_part, "dp", scatter_dimension=0, tiled=True)

    in_grad = lax.dot_general(
        tok_sel_b, arrived, (((0, 1), (0, 1)), ((), ())), preferred_element_type=f32
    ).astype(bf16)
    weight_block = jnp.concatenate([in_block, down_block], axis=1)
    return (in_grad, weight_block[None])


def solution(mesh):
    return jax.shard_map(
        per_device,
        mesh=mesh,
        in_specs=(
            P(("dp", "expert"), None),
            P(("dp", "expert"), None),
            P(("dp", "expert"), None),
            P(("dp", "expert"), None),
            P(),
            P("expert", None, None),
            P("expert", None, None),
            P("dp", "expert", None, None),
        ),
        out_specs=(P(("dp", "expert"), None), P("expert", "dp", None)),
        check_vma=False,
    )
```

```python
import jax
import jax.numpy as jnp
from jax import lax
from jax.experimental.layout import Layout, with_layout_constraint
from jax.sharding import PartitionSpec as P


def row_major(x):
    return with_layout_constraint(x, Layout(major_to_minor=tuple(range(x.ndim))))


def col_major(x):
    return with_layout_constraint(x, Layout(major_to_minor=(1, 0)))


def per_device(tokens, out_grad, expert_ids, gate_weights, trained, w_in, w_down, saved):
    groups = lax.axis_size("expert")
    local_count = w_in.shape[0]
    experts = local_count * groups
    tok_count = tokens.shape[0]
    fanout = expert_ids.shape[1]
    slot_total = saved.shape[2]
    capacity = slot_total // groups
    hidden_units = w_down.shape[1]
    f32, bf16 = jnp.float32, jnp.bfloat16

    flat_ids = expert_ids.reshape(-1)
    entries = flat_ids.shape[0]
    onehot = (flat_ids[:, None] == jnp.arange(experts, dtype=jnp.int32)[None, :]).astype(bf16)
    order = jnp.arange(entries, dtype=jnp.int32)
    earlier = (order[:, None] > order[None, :]).astype(bf16)
    before = lax.dot_general(earlier, onehot, (((1,), (0,)), ((), ())), preferred_element_type=f32)
    slot_rank = jnp.sum(before * onehot.astype(f32), axis=1).astype(jnp.int32)
    ids4 = flat_ids.reshape(1, 1, tok_count, fanout)
    rank4 = slot_rank.reshape(1, 1, tok_count, fanout)
    sel = (ids4 == jnp.arange(experts, dtype=jnp.int32)[:, None, None, None]) & (
        rank4 == jnp.arange(capacity, dtype=jnp.int32)[None, :, None, None]
    )
    tok_sel = jnp.any(sel, axis=3)
    tok_sel_b = tok_sel.astype(bf16)
    gate_slot = jnp.sum(jnp.where(sel, gate_weights[None, None, :, :], 0.0), axis=(2, 3))

    pick = (((2,), (0,)), ((), ()))
    og_slot = lax.dot_general(tok_sel_b, out_grad, pick, preferred_element_type=f32)
    s_send = (gate_slot[:, :, None] * og_slot).astype(bf16)
    lanes = 128
    rows = tokens.shape[1] // lanes
    slot_tok = jnp.sum(jnp.where(tok_sel, jnp.arange(tok_count, dtype=jnp.int32), 0), axis=2)
    filled = jnp.any(tok_sel, axis=2).reshape(-1)
    tok3 = tokens.reshape(tok_count, rows, lanes)
    x_send = jnp.where(filled[:, None, None], tok3[slot_tok.reshape(-1)], jnp.zeros((), bf16))
    x_send = x_send.reshape(groups, capacity * rows, lanes)

    saved3 = saved.reshape(groups, capacity, 2 * hidden_units)
    gate_pre = saved3[:, :, :hidden_units].astype(f32)
    up_pre = saved3[:, :, hidden_units:].astype(f32)
    sigmoid_gate = jax.nn.sigmoid(gate_pre)
    activated = gate_pre * sigmoid_gate
    hidden = (activated * up_pre).astype(bf16)

    s_recv = lax.all_to_all(row_major(s_send), "expert", 0, 0, tiled=True)
    x_send, s_recv, hidden = lax.optimization_barrier((x_send, s_recv, hidden))
    x_recv = lax.all_to_all(row_major(x_send), "expert", 0, 0, tiled=True)

    trained_flag = jnp.any(trained == lax.axis_index("expert")).astype(f32)
    over_slots = (((0, 1), (0, 1)), ((), ()))
    grad_down = lax.dot_general(s_recv, hidden, over_slots, preferred_element_type=f32)
    down_part = col_major((grad_down * trained_flag).astype(bf16))
    down_part, s_recv = lax.optimization_barrier((down_part, s_recv))
    down_block = lax.psum_scatter(down_part, "dp", scatter_dimension=0, tiled=True)

    hidden_grad = lax.dot_general(
        s_recv, w_down[0], (((2,), (1,)), ((), ())), preferred_element_type=f32
    )
    pre_grad = jnp.concatenate(
        [
            hidden_grad * up_pre * sigmoid_gate * (1.0 + gate_pre * (1.0 - sigmoid_gate)),
            hidden_grad * activated,
        ],
        axis=2,
    ).astype(bf16)
    slot_grads = lax.dot_general(
        pre_grad, w_in[0], (((2,), (1,)), ((), ())), preferred_element_type=f32
    ).astype(bf16)

    slot_grads, x_recv = lax.optimization_barrier((slot_grads, x_recv))
    arrived = lax.all_to_all(row_major(slot_grads), "expert", 0, 0, tiled=True)

    x_rows = x_recv.reshape(groups * capacity, rows, lanes)
    pre_rows = pre_grad.reshape(groups * capacity, 2 * hidden_units)
    grad_in = lax.dot_general(x_rows, pre_rows, (((0,), (0,)), ((), ())), preferred_element_type=f32)
    in_part = (grad_in.reshape(rows * lanes, 2 * hidden_units) * trained_flag).astype(bf16)
    in_block = lax.psum_scatter(in_part, "dp", scatter_dimension=0, tiled=True)

    in_grad = lax.dot_general(
        tok_sel_b, arrived, (((0, 1), (0, 1)), ((), ())), preferred_element_type=f32
    ).astype(bf16)
    weight_block = jnp.concatenate([in_block, down_block], axis=1)[None]
    weight_block = with_layout_constraint(weight_block, Layout(major_to_minor=(0, 2, 1)))
    return (in_grad, weight_block)


def solution(mesh):
    return jax.shard_map(
        per_device,
        mesh=mesh,
        in_specs=(
            P(("dp", "expert"), None),
            P(("dp", "expert"), None),
            P(("dp", "expert"), None),
            P(("dp", "expert"), None),
            P(),
            P("expert", None, None),
            P("expert", None, None),
            P("dp", "expert", None, None),
        ),
        out_specs=(P(("dp", "expert"), None), P("expert", "dp", None)),
        check_vma=False,
    )
```

```python
import jax
import jax.numpy as jnp
from jax import lax
from jax.experimental.layout import Layout, with_layout_constraint
from jax.sharding import PartitionSpec as P


def row_major(x):
    return with_layout_constraint(x, Layout(major_to_minor=tuple(range(x.ndim))))


def col_major(x):
    return with_layout_constraint(x, Layout(major_to_minor=(1, 0)))


def per_device(tokens, out_grad, expert_ids, gate_weights, trained, w_in, w_down, saved):
    groups = lax.axis_size("expert")
    local_count = w_in.shape[0]
    experts = local_count * groups
    tok_count = tokens.shape[0]
    fanout = expert_ids.shape[1]
    slot_total = saved.shape[2]
    capacity = slot_total // groups
    hidden_units = w_down.shape[1]
    f32, bf16 = jnp.float32, jnp.bfloat16

    flat_ids = expert_ids.reshape(-1)
    entries = flat_ids.shape[0]
    onehot = (flat_ids[:, None] == jnp.arange(experts, dtype=jnp.int32)[None, :]).astype(bf16)
    order = jnp.arange(entries, dtype=jnp.int32)
    earlier = (order[:, None] > order[None, :]).astype(bf16)
    before = lax.dot_general(earlier, onehot, (((1,), (0,)), ((), ())), preferred_element_type=f32)
    slot_rank = jnp.sum(before * onehot.astype(f32), axis=1).astype(jnp.int32)
    ids4 = flat_ids.reshape(1, 1, tok_count, fanout)
    rank4 = slot_rank.reshape(1, 1, tok_count, fanout)
    sel = (ids4 == jnp.arange(experts, dtype=jnp.int32)[:, None, None, None]) & (
        rank4 == jnp.arange(capacity, dtype=jnp.int32)[None, :, None, None]
    )
    tok_sel = jnp.any(sel, axis=3)
    tok_sel_b = tok_sel.astype(bf16)
    gate_slot = jnp.sum(jnp.where(sel, gate_weights[None, None, :, :], 0.0), axis=(2, 3))

    pick = (((2,), (0,)), ((), ()))
    lanes = 128
    rows = tokens.shape[1] // lanes
    slot_count = groups * capacity
    og3 = out_grad.reshape(tok_count, rows, lanes)
    og_slot = lax.dot_general(tok_sel_b, og3, pick, preferred_element_type=f32)
    s_send = (gate_slot[:, :, None, None] * og_slot).astype(bf16)
    s_send = s_send.reshape(groups, capacity * rows, lanes)
    slot_tok = jnp.sum(jnp.where(tok_sel, jnp.arange(tok_count, dtype=jnp.int32), 0), axis=2)
    filled = jnp.any(tok_sel, axis=2).reshape(-1)
    tok3 = tokens.reshape(tok_count, rows, lanes)
    x_send = jnp.where(filled[:, None, None], tok3[slot_tok.reshape(-1)], jnp.zeros((), bf16))
    x_send = x_send.reshape(groups, capacity * rows, lanes)

    saved3 = saved.reshape(groups, capacity, 2 * hidden_units)
    saved_rows = saved.reshape(slot_count, 2 * hidden_units)
    gate_rows = saved_rows[:, :hidden_units].astype(f32)
    activated_rows = gate_rows * jax.nn.sigmoid(gate_rows)
    hidden_rows = (activated_rows * saved_rows[:, hidden_units:].astype(f32)).astype(bf16)

    s_recv = lax.all_to_all(row_major(s_send), "expert", 0, 0, tiled=True)
    x_send, s_recv, hidden_rows, saved3 = lax.optimization_barrier(
        (x_send, s_recv, hidden_rows, saved3)
    )
    x_recv = lax.all_to_all(row_major(x_send), "expert", 0, 0, tiled=True)

    trained_flag = jnp.any(trained == lax.axis_index("expert")).astype(f32)
    over_slots = (((0, 1), (0, 1)), ((), ()))
    grad_down = lax.dot_general(
        s_recv.reshape(slot_count, rows, lanes), hidden_rows, (((0,), (0,)), ((), ())),
        preferred_element_type=f32,
    )
    down_part = (grad_down.reshape(rows * lanes, hidden_units) * trained_flag).astype(bf16)
    down_part = col_major(down_part)
    down_part, s_recv = lax.optimization_barrier((down_part, s_recv))
    s_recv = s_recv.reshape(groups, capacity, rows * lanes)
    down_block = lax.psum_scatter(down_part, "dp", scatter_dimension=0, tiled=True)

    gate_pre = saved3[:, :, :hidden_units].astype(f32)
    up_pre = saved3[:, :, hidden_units:].astype(f32)
    sigmoid_gate = jax.nn.sigmoid(gate_pre)
    activated = gate_pre * sigmoid_gate
    hidden_grad = lax.dot_general(
        s_recv, w_down[0], (((2,), (1,)), ((), ())), preferred_element_type=f32
    )
    pre_grad = jnp.concatenate(
        [
            hidden_grad * up_pre * sigmoid_gate * (1.0 + gate_pre * (1.0 - sigmoid_gate)),
            hidden_grad * activated,
        ],
        axis=2,
    ).astype(bf16)
    slot_grads = lax.dot_general(
        pre_grad, w_in[0], (((2,), (1,)), ((), ())), preferred_element_type=f32
    ).astype(bf16)

    slot_grads, x_recv = lax.optimization_barrier((slot_grads, x_recv))
    arrived = lax.all_to_all(row_major(slot_grads), "expert", 0, 0, tiled=True)

    x_rows = x_recv.reshape(groups * capacity, rows, lanes)
    pre_rows = pre_grad.reshape(groups * capacity, 2 * hidden_units)
    grad_in = lax.dot_general(x_rows, pre_rows, (((0,), (0,)), ((), ())), preferred_element_type=f32)
    in_part = (grad_in.reshape(rows * lanes, 2 * hidden_units) * trained_flag).astype(bf16)
    in_block = lax.psum_scatter(in_part, "dp", scatter_dimension=0, tiled=True)

    in_grad = lax.dot_general(
        tok_sel_b, arrived, (((0, 1), (0, 1)), ((), ())), preferred_element_type=f32
    ).astype(bf16)
    weight_block = jnp.concatenate([in_block, down_block], axis=1)[None]
    weight_block = with_layout_constraint(weight_block, Layout(major_to_minor=(0, 2, 1)))
    return (in_grad, weight_block)


def solution(mesh):
    return jax.shard_map(
        per_device,
        mesh=mesh,
        in_specs=(
            P(("dp", "expert"), None),
            P(("dp", "expert"), None),
            P(("dp", "expert"), None),
            P(("dp", "expert"), None),
            P(),
            P("expert", None, None),
            P("expert", None, None),
            P("dp", "expert", None, None),
        ),
        out_specs=(P(("dp", "expert"), None), P("expert", "dp", None)),
        check_vma=False,
    )
```

```python
import jax
import jax.numpy as jnp
from jax import lax
from jax.experimental.layout import Layout, with_layout_constraint
from jax.sharding import PartitionSpec as P


def row_major(x):
    return with_layout_constraint(x, Layout(major_to_minor=tuple(range(x.ndim))))


def col_major(x):
    return with_layout_constraint(x, Layout(major_to_minor=(1, 0)))


def per_device(tokens, out_grad, expert_ids, gate_weights, trained, w_in, w_down, saved):
    groups = lax.axis_size("expert")
    local_count = w_in.shape[0]
    experts = local_count * groups
    tok_count = tokens.shape[0]
    fanout = expert_ids.shape[1]
    slot_total = saved.shape[2]
    capacity = slot_total // groups
    hidden_units = w_down.shape[1]
    f32, bf16 = jnp.float32, jnp.bfloat16

    labels = jnp.arange(experts, dtype=jnp.int32)
    hit = expert_ids[:, :, None] == labels[None, None, :]
    tok_mask = jnp.any(hit, axis=1)
    tok_gate = jnp.sum(jnp.where(hit, gate_weights[:, :, None], 0.0), axis=1)
    order = jnp.arange(tok_count, dtype=jnp.int32)
    earlier = (order[:, None] > order[None, :]).astype(bf16)
    before = lax.dot_general(
        earlier, tok_mask.astype(bf16), (((1,), (0,)), ((), ())), preferred_element_type=f32
    ).astype(jnp.int32)
    tok_sel = tok_mask.T[:, None, :] & (
        before.T[:, None, :] == jnp.arange(capacity, dtype=jnp.int32)[None, :, None]
    )
    tok_sel_b = tok_sel.astype(bf16)
    gate_slot = jnp.sum(jnp.where(tok_sel, tok_gate.T[:, None, :], 0.0), axis=2)

    pick = (((2,), (0,)), ((), ()))
    lanes = 128
    rows = tokens.shape[1] // lanes
    slot_count = groups * capacity
    og3 = out_grad.reshape(tok_count, rows, lanes)
    og_slot = lax.dot_general(tok_sel_b, og3, pick, preferred_element_type=f32)
    s_send = (gate_slot[:, :, None, None] * og_slot).astype(bf16)
    s_send = s_send.reshape(groups, capacity * rows, lanes)
    slot_tok = jnp.sum(jnp.where(tok_sel, jnp.arange(tok_count, dtype=jnp.int32), 0), axis=2)
    filled = jnp.any(tok_sel, axis=2).reshape(-1)
    tok3 = tokens.reshape(tok_count, rows, lanes)
    x_send = jnp.where(filled[:, None, None], tok3[slot_tok.reshape(-1)], jnp.zeros((), bf16))
    x_send = x_send.reshape(groups, capacity * rows, lanes)

    saved3 = saved.reshape(groups, capacity, 2 * hidden_units)
    saved_rows = saved.reshape(slot_count, 2 * hidden_units)
    gate_rows = saved_rows[:, :hidden_units].astype(f32)
    activated_rows = gate_rows * jax.nn.sigmoid(gate_rows)
    hidden_rows = (activated_rows * saved_rows[:, hidden_units:].astype(f32)).astype(bf16)

    s_recv = lax.all_to_all(row_major(s_send), "expert", 0, 0, tiled=True)
    x_send, s_recv, hidden_rows, saved3 = lax.optimization_barrier(
        (x_send, s_recv, hidden_rows, saved3)
    )
    x_recv = lax.all_to_all(row_major(x_send), "expert", 0, 0, tiled=True)

    trained_flag = jnp.any(trained == lax.axis_index("expert")).astype(f32)
    over_slots = (((0, 1), (0, 1)), ((), ()))
    grad_down = lax.dot_general(
        s_recv.reshape(slot_count, rows, lanes), hidden_rows, (((0,), (0,)), ((), ())),
        preferred_element_type=f32,
    )
    down_part = (grad_down.reshape(rows * lanes, hidden_units) * trained_flag).astype(bf16)
    down_part = col_major(down_part)
    down_part, s_recv = lax.optimization_barrier((down_part, s_recv))
    s_recv = s_recv.reshape(groups, capacity, rows * lanes)
    down_block = lax.psum_scatter(down_part, "dp", scatter_dimension=0, tiled=True)

    gate_pre = saved3[:, :, :hidden_units].astype(f32)
    up_pre = saved3[:, :, hidden_units:].astype(f32)
    sigmoid_gate = jax.nn.sigmoid(gate_pre)
    activated = gate_pre * sigmoid_gate
    hidden_grad = lax.dot_general(
        s_recv, w_down[0], (((2,), (1,)), ((), ())), preferred_element_type=f32
    )
    pre_grad = jnp.concatenate(
        [
            hidden_grad * up_pre * sigmoid_gate * (1.0 + gate_pre * (1.0 - sigmoid_gate)),
            hidden_grad * activated,
        ],
        axis=2,
    ).astype(bf16)
    slot_grads = lax.dot_general(
        pre_grad, w_in[0], (((2,), (1,)), ((), ())), preferred_element_type=f32
    ).astype(bf16)

    slot_grads, x_recv = lax.optimization_barrier((slot_grads, x_recv))
    arrived = lax.all_to_all(row_major(slot_grads), "expert", 0, 0, tiled=True)

    x_rows = x_recv.reshape(groups * capacity, rows, lanes)
    pre_rows = pre_grad.reshape(groups * capacity, 2 * hidden_units)
    grad_in = lax.dot_general(x_rows, pre_rows, (((0,), (0,)), ((), ())), preferred_element_type=f32)
    in_part = (grad_in.reshape(rows * lanes, 2 * hidden_units) * trained_flag).astype(bf16)
    in_block = lax.psum_scatter(in_part, "dp", scatter_dimension=0, tiled=True)

    in_grad = lax.dot_general(
        tok_sel_b, arrived, (((0, 1), (0, 1)), ((), ())), preferred_element_type=f32
    ).astype(bf16)
    weight_block = jnp.concatenate([in_block, down_block], axis=1)[None]
    weight_block = with_layout_constraint(weight_block, Layout(major_to_minor=(0, 2, 1)))
    return (in_grad, weight_block)


def solution(mesh):
    return jax.shard_map(
        per_device,
        mesh=mesh,
        in_specs=(
            P(("dp", "expert"), None),
            P(("dp", "expert"), None),
            P(("dp", "expert"), None),
            P(("dp", "expert"), None),
            P(),
            P("expert", None, None),
            P("expert", None, None),
            P("dp", "expert", None, None),
        ),
        out_specs=(P(("dp", "expert"), None), P("expert", "dp", None)),
        check_vma=False,
    )
```

```python
import jax
import jax.numpy as jnp
from jax import lax
from jax.experimental.layout import Layout, with_layout_constraint
from jax.sharding import PartitionSpec as P


def row_major(x):
    return with_layout_constraint(x, Layout(major_to_minor=tuple(range(x.ndim))))


def col_major(x):
    return with_layout_constraint(x, Layout(major_to_minor=(1, 0)))


def per_device(tokens, out_grad, expert_ids, gate_weights, trained, w_in, w_down, saved):
    groups = lax.axis_size("expert")
    local_count = w_in.shape[0]
    experts = local_count * groups
    tok_count = tokens.shape[0]
    fanout = expert_ids.shape[1]
    slot_total = saved.shape[2]
    capacity = slot_total // groups
    hidden_units = w_down.shape[1]
    f32, bf16 = jnp.float32, jnp.bfloat16

    labels = jnp.arange(experts, dtype=jnp.int32)
    hit = expert_ids[:, :, None] == labels[None, None, :]
    tok_mask = jnp.any(hit, axis=1)
    tok_gate = jnp.sum(jnp.where(hit, gate_weights[:, :, None], 0.0), axis=1)
    order = jnp.arange(tok_count, dtype=jnp.int32)
    earlier = (order[:, None] > order[None, :]).astype(bf16)
    before = lax.dot_general(
        earlier, tok_mask.astype(bf16), (((1,), (0,)), ((), ())), preferred_element_type=f32
    ).astype(jnp.int32)
    tok_sel = tok_mask.T[:, None, :] & (
        before.T[:, None, :] == jnp.arange(capacity, dtype=jnp.int32)[None, :, None]
    )
    tok_sel_b = tok_sel.astype(bf16)
    gate_slot = jnp.sum(jnp.where(tok_sel, tok_gate.T[:, None, :], 0.0), axis=2)

    pick = (((2,), (0,)), ((), ()))
    lanes = 128
    rows = tokens.shape[1] // lanes
    slot_count = groups * capacity
    og3 = out_grad.reshape(tok_count, rows, lanes)
    og_slot = lax.dot_general(tok_sel_b, og3, pick, preferred_element_type=f32)
    s_send = (gate_slot[:, :, None, None] * og_slot).astype(bf16)
    s_send = s_send.reshape(groups, capacity * rows, lanes)
    slot_tok = jnp.sum(jnp.where(tok_sel, jnp.arange(tok_count, dtype=jnp.int32), 0), axis=2)
    filled = jnp.any(tok_sel, axis=2).reshape(-1)
    tok3 = tokens.reshape(tok_count, rows, lanes)
    x_send = jnp.where(filled[:, None, None], tok3[slot_tok.reshape(-1)], jnp.zeros((), bf16))
    x_send = x_send.reshape(groups, capacity * rows, lanes)

    saved3 = saved.reshape(groups, capacity, 2 * hidden_units)
    saved_rows = saved.reshape(slot_count, 2 * hidden_units)
    gate_rows = saved_rows[:, :hidden_units].astype(f32)
    activated_rows = gate_rows * jax.nn.sigmoid(gate_rows)
    hidden_rows = (activated_rows * saved_rows[:, hidden_units:].astype(f32)).astype(bf16)

    s_recv = lax.all_to_all(row_major(s_send), "expert", 0, 0, tiled=True)
    x_send, s_recv, hidden_rows, saved3 = lax.optimization_barrier(
        (x_send, s_recv, hidden_rows, saved3)
    )
    x_recv = lax.all_to_all(row_major(x_send), "expert", 0, 0, tiled=True)

    trained_flag = jnp.any(trained == lax.axis_index("expert")).astype(f32)
    over_slots = (((0, 1), (0, 1)), ((), ()))
    grad_down = lax.dot_general(
        s_recv.reshape(slot_count, rows, lanes), hidden_rows, (((0,), (0,)), ((), ())),
        preferred_element_type=f32,
    )
    down_part = (grad_down.reshape(rows * lanes, hidden_units) * trained_flag).astype(bf16)
    down_part = col_major(down_part)
    down_part, s_recv = lax.optimization_barrier((down_part, s_recv))
    s_recv = s_recv.reshape(groups, capacity, rows * lanes)
    down_block = lax.psum_scatter(down_part, "dp", scatter_dimension=0, tiled=True)

    gate_pre = saved3[:, :, :hidden_units].astype(f32)
    up_pre = saved3[:, :, hidden_units:].astype(f32)
    sigmoid_gate = jax.nn.sigmoid(gate_pre)
    activated = gate_pre * sigmoid_gate
    hidden_grad = lax.dot_general(
        s_recv, w_down[0], (((2,), (1,)), ((), ())), preferred_element_type=f32
    )
    pre_grad = jnp.concatenate(
        [
            hidden_grad * up_pre * sigmoid_gate * (1.0 + gate_pre * (1.0 - sigmoid_gate)),
            hidden_grad * activated,
        ],
        axis=2,
    ).astype(bf16)
    slot_grads = lax.dot_general(
        pre_grad, w_in[0], (((2,), (1,)), ((), ())), preferred_element_type=f32
    ).astype(bf16)

    slot_grads, x_recv = lax.optimization_barrier((slot_grads, x_recv))
    arrived = lax.all_to_all(row_major(slot_grads), "expert", 0, 0, tiled=True)

    x_rows = x_recv.reshape(groups * capacity, rows, lanes)
    pre_rows = pre_grad.reshape(groups * capacity, 2 * hidden_units)
    grad_in = lax.dot_general(x_rows, pre_rows, (((0,), (0,)), ((), ())), preferred_element_type=f32)
    in_part = (grad_in.reshape(rows * lanes, 2 * hidden_units) * trained_flag).astype(bf16)
    in_block = lax.psum_scatter(in_part, "dp", scatter_dimension=0, tiled=True)

    in_grad = lax.dot_general(
        tok_sel_b, arrived, (((0, 1), (0, 1)), ((), ())), preferred_element_type=f32
    ).astype(bf16)
    layout = Layout(major_to_minor=(0, 2, 1))
    frame = jnp.concatenate([jnp.zeros_like(in_block), down_block], axis=1)[None]
    frame = with_layout_constraint(frame, layout)
    weight_block = lax.dynamic_update_slice(frame, in_block[None], (0, 0, 0))
    weight_block = with_layout_constraint(weight_block, layout)
    return (in_grad, weight_block)


def solution(mesh):
    return jax.shard_map(
        per_device,
        mesh=mesh,
        in_specs=(
            P(("dp", "expert"), None),
            P(("dp", "expert"), None),
            P(("dp", "expert"), None),
            P(("dp", "expert"), None),
            P(),
            P("expert", None, None),
            P("expert", None, None),
            P("dp", "expert", None, None),
        ),
        out_specs=(P(("dp", "expert"), None), P("expert", "dp", None)),
        check_vma=False,
    )
```
